32 devices in a mesh: dp: 8 (over y, x, core), tensor: 4 (over z).
Axes of the slice: x: 2, y: 2, z: 4, core: 2. Of those that a mesh axis runs over, the one named last changes fastest.
Arguments:
- tokens: bfloat16 [16, 577, 1024], P('dp', None, 'tensor'), may hold values from -6 to 6
- cotangent: float32 [16, 577, 1024], P('dp', None, 'tensor'), may hold values from -6 to 6
- image_counts: int32 [8], P('dp'), may hold values from 1 to 2, as said below
- w_qkv: float32 [2, 1024, 3, 1024], P(None, 'dp', None, 'tensor'), as said below
- w_out: float32 [2, 1024, 1024], P(None, 'dp', 'tensor'), may hold values from -0.75 to 0.75
- w_fc1: float32 [2, 1024, 4096], P(None, 'dp', 'tensor'), may hold values from -0.1875 to 0.1875
- w_fc2: float32 [2, 1024, 4096], P(None, 'dp', 'tensor'), may hold values from -0.09375 to 0.09375
- vec_small: float32 [2, 8, 1024], P(None, None, 'tensor'), as said below
- fc1_bias: float32 [2, 4096], P(None, 'tensor'), may hold values from -3 to 3
- mom_qkv: float32 [2, 2, 1024, 3, 1024], P(None, None, 'dp', None, 'tensor'), as said below
- mom_out: float32 [2, 2, 1024, 1024], P(None, None, 'dp', 'tensor'), as said below
- mom_fc1: float32 [2, 2, 1024, 4096], P(None, None, 'dp', 'tensor'), as said below
- mom_fc2: float32 [2, 2, 1024, 4096], P(None, None, 'dp', 'tensor'), as said below
- mom_vec: float32 [2, 2, 8, 1024], P(None, None, None, 'tensor'), as said below
- mom_bias: float32 [2, 2, 4096], P(None, None, 'tensor'), as said below
Outputs:
- output: float32 [16, 577, 1024], P('dp', None, 'tensor')
- input_grad: float32 [16, 577, 1024], P('dp', None, 'tensor')
- grad_qkv: float32 [2, 1024, 3, 1024], P(None, 'dp', None, 'tensor')
- grad_out: float32 [2, 1024, 1024], P(None, 'dp', 'tensor')
- grad_fc1: float32 [2, 1024, 4096], P(None, 'dp', 'tensor')
- grad_fc2: float32 [2, 1024, 4096], P(None, 'dp', 'tensor')
- grad_vec: float32 [2, 8, 1024], P(None, None, 'tensor')
- grad_bias: float32 [2, 4096], P(None, 'tensor')
- new_qkv: float32 [2, 1024, 3, 1024], P(None, 'dp', None, 'tensor')
- new_out: float32 [2, 1024, 1024], P(None, 'dp', 'tensor')
- new_fc1: float32 [2, 1024, 4096], P(None, 'dp', 'tensor')
- new_fc2: float32 [2, 1024, 4096], P(None, 'dp', 'tensor')
- new_vec: float32 [2, 8, 1024], P(None, None, 'tensor')
- new_bias: float32 [2, 4096], P(None, 'tensor')
- newmom_qkv: float32 [2, 2, 1024, 3, 1024], P(None, None, 'dp', None, 'tensor')
- newmom_out: float32 [2, 2, 1024, 1024], P(None, None, 'dp', 'tensor')
- newmom_fc1: float32 [2, 2, 1024, 4096], P(None, None, 'dp', 'tensor')
- newmom_fc2: float32 [2, 2, 1024, 4096], P(None, None, 'dp', 'tensor')
- newmom_vec: float32 [2, 2, 8, 1024], P(None, None, None, 'tensor')
- newmom_bias: float32 [2, 2, 4096], P(None, None, 'tensor')
The draws below stay inside these ranges and needn't reach their ends.
Inputs may be any that keep to these rules, and one draw needn't show every extreme that they name: Every index of dp holds 1 or 2 images; some index holds 2 and some holds 1. Slot 2 i always holds an image, slot 2 i + 1 only where image_counts[i] is 2; other slots' tokens and cotangents are ignored. `w_qkv`: independent entries of mean 0 and deviation 1024^-0.5. `vec_small`: gains and shifts of order one. `mom_qkv`: second moments (index 1 of dimension 0) are positive. `mom_out`: second moments (index 1 of dimension 0) are positive. `mom_fc1`: second moments (index 1 of dimension 0) are positive. `mom_fc2`: second moments (index 1 of dimension 0) are positive. `mom_vec`: second moments (index 1 of dimension 0) are positive. `mom_bias`: second moments (index 1 of dimension 0) are positive.
All inputs are finite; a program needn't handle non-finite values.
Results may differ from the reference program's by a relative error of at most 0.022.
Values may be sent and summed in bfloat16 or wider, within the bound.
A program may use at most 256 MiB of HBM per device.

```python
import math
import jax
import jax.numpy as jnp
from jax import lax

D = 1024
HEADS = 16
FF = 4096
SEQ = 577
LAYERS = 2
STEP = 10
HD = 64
SLOTS = 16


def draw_image_counts(key, part):
    device_total = SLOTS // 2
    key_one, key_two, key_three = jax.random.split(key, 3)
    counts = jax.random.randint(key_one, (device_total,), 1, 3)
    busy_index = jax.random.randint(key_two, (), 0, device_total)
    light_index = (busy_index + 1 + jax.random.randint(key_three, (), 0, device_total - 1)) % device_total
    positions = jnp.arange(device_total)
    counts = jnp.where(positions == busy_index, 2, counts)
    counts = jnp.where(positions == light_index, 1, counts)
    return counts.astype(jnp.int32)


def draw_w_qkv(key, part):
    key_one = jax.random.fold_in(key, 0)
    base = jax.random.normal(key_one, (LAYERS, D, 3, D), jnp.float32) * D ** (-0.5)
    return base


def draw_vec_small(key, part):
    key_one, key_two = jax.random.split(key)
    raw_rows = jax.random.normal(key_one, (LAYERS, 8, D), jnp.float32) * 0.5
    gains = jnp.exp(jax.random.uniform(key_two, (LAYERS, 8, D), jnp.float32, -0.7, 0.7))
    row_index = jnp.arange(8)[None, :, None]
    return jnp.where((row_index == 0) | (row_index == 5), gains, raw_rows)


def second_level():
    return 0.0005 * (D / max(D // 16, 1)) * SLOTS * SEQ


def moment_pair(key, shape, level):
    key_one, key_two = jax.random.split(key)
    first = jax.random.normal(key_one, shape, jnp.float32) * 2.0
    second = level * jnp.exp(jax.random.uniform(key_two, shape, jnp.float32, math.log(0.3), math.log(3.0)))
    return jnp.stack([first, second])


def draw_mom_qkv(key, part):
    return moment_pair(jax.random.fold_in(key, 11), (LAYERS, D, 3, D), second_level())


def draw_mom_out(key, part):
    return moment_pair(jax.random.fold_in(key, 12), (LAYERS, D, D), 1.0)


def draw_mom_fc1(key, part):
    return moment_pair(jax.random.fold_in(key, 13), (LAYERS, D, FF), 1.0)


def draw_mom_fc2(key, part):
    return moment_pair(jax.random.fold_in(key, 14), (LAYERS, D, FF), 1.0)


def draw_mom_vec(key, part):
    return moment_pair(jax.random.fold_in(key, 15), (LAYERS, 8, D), second_level())


def draw_mom_bias(key, part):
    return moment_pair(jax.random.fold_in(key, 16), (LAYERS, FF), 1.0)


def shard_levels(key, extent, shards, low, high):
    def one(dim, shards_of):
        steps = jax.random.uniform(jax.random.fold_in(jax.random.fold_in(key, 6), dim), (shards_of,), jnp.float32, low / len(shards), high / len(shards))
        return jnp.repeat(jnp.exp(steps), extent[dim] // shards_of).reshape((-1,) + (1,) * (len(extent) - dim - 1))

    level = one(*shards[0])
    for cut in shards[1:]:
        level = level * one(*cut)
    return level


def centred(rng, dims, width, limit, pieces=(), dtype=jnp.bfloat16):
    entries = jax.random.normal(rng, dims, jnp.float32) * width
    if len(pieces) > 0:
        entries = shard_levels(rng, dims, pieces, -0.22, 0.18) * entries
    return jnp.clip(entries, min=-limit, max=limit).astype(dtype)


def setup_inputs(seed: int = 0) -> dict:
    arg_keys = jax.random.split(jax.random.key(seed), 16)
    tokens = centred(arg_keys[0], (SLOTS, SEQ, D), 1.0, 6.0, ((0, 8), (2, 4)))
    cotangent = centred(arg_keys[1], (SLOTS, SEQ, D), 1.0, 6.0, ((0, 8), (2, 4)), jnp.float32)
    image_counts = draw_image_counts(jax.random.fold_in(arg_keys[15], 71), 0)
    w_qkv = draw_w_qkv(jax.random.fold_in(arg_keys[15], 71), 0)
    w_out = centred(arg_keys[4], (LAYERS, D, D), (max(D // 16, 1)) ** -0.5, 0.75, ((1, 8), (2, 4)), jnp.float32)
    w_fc1 = centred(arg_keys[5], (LAYERS, D, FF), D ** -0.5, 0.1875, ((1, 8), (2, 4)), jnp.float32)
    w_fc2 = centred(arg_keys[6], (LAYERS, D, FF), FF ** -0.5, 0.09375, ((1, 8), (2, 4)), jnp.float32)
    vec_small = draw_vec_small(jax.random.fold_in(arg_keys[15], 71), 0)
    fc1_bias = centred(arg_keys[8], (LAYERS, FF), 0.5, 3.0, ((1, 4),), jnp.float32)
    mom_qkv = draw_mom_qkv(jax.random.fold_in(arg_keys[15], 71), 0)
    mom_out = draw_mom_out(jax.random.fold_in(arg_keys[15], 71), 0)
    mom_fc1 = draw_mom_fc1(jax.random.fold_in(arg_keys[15], 71), 0)
    mom_fc2 = draw_mom_fc2(jax.random.fold_in(arg_keys[15], 71), 0)
    mom_vec = draw_mom_vec(jax.random.fold_in(arg_keys[15], 71), 0)
    mom_bias = draw_mom_bias(jax.random.fold_in(arg_keys[15], 71), 0)
    return dict(tokens=tokens, cotangent=cotangent, image_counts=image_counts, w_qkv=w_qkv, w_out=w_out, w_fc1=w_fc1, w_fc2=w_fc2, vec_small=vec_small, fc1_bias=fc1_bias, mom_qkv=mom_qkv, mom_out=mom_out, mom_fc1=mom_fc1, mom_fc2=mom_fc2, mom_vec=mom_vec, mom_bias=mom_bias)


NORM_EPS = 1e-06
ROOT_HALF = 0.7071067811865476
INV_ROOT_TWO_PI = 0.3989422804014327
LEARN_RATE = 0.01
BETA_ONE = 0.9
BETA_TWO = 0.999
ADAM_EPS = 1e-08
WEIGHT_DECAY = 0.05

def gelu_value(preactivation):
    return 0.5 * preactivation * (1.0 + jax.scipy.special.erf(preactivation * ROOT_HALF))

def gelu_slope(preactivation):
    return 0.5 * (1.0 + jax.scipy.special.erf(preactivation * ROOT_HALF)) + preactivation * jnp.exp(-0.5 * preactivation * preactivation) * INV_ROOT_TWO_PI

def layernorm_forward(hidden_state):
    mean_row = lax.optimization_barrier(jnp.mean(hidden_state, -1, keepdims=True))
    spread = lax.optimization_barrier(jnp.mean(hidden_state * hidden_state, -1, keepdims=True)) - mean_row * mean_row
    inv_std = lax.rsqrt(spread + NORM_EPS)
    return ((hidden_state - mean_row) * inv_std, inv_std)

def layernorm_backward(d_normed, normed, inv_std, gain, carried):
    d_hat = d_normed * gain
    grad_in = carried + inv_std * (d_hat - lax.optimization_barrier(jnp.mean(d_hat, -1, keepdims=True)) - normed * lax.optimization_barrier(jnp.mean(d_hat * normed, -1, keepdims=True)))
    return (grad_in, lax.optimization_barrier(jnp.sum(d_normed * normed, 0)), lax.optimization_barrier(jnp.sum(d_normed, 0)))

def split_heads(matrix):
    return matrix.reshape(matrix.shape[0], HEADS, HD)

def attend_forward(query_h, key_h, value_h):
    scores = jnp.einsum('qhd,khd->hqk', query_h.astype(jnp.float32), key_h.astype(jnp.float32)) * HD ** (-0.5)
    top_score = lax.optimization_barrier(jnp.max(scores, -1, keepdims=True))
    logged_total = top_score + jnp.log(lax.optimization_barrier(jnp.sum(jnp.exp(scores - top_score), -1, keepdims=True)))
    probs = jnp.exp(scores - logged_total).astype(jnp.bfloat16)
    attention_result = jnp.einsum('hqk,khd->qhd', probs.astype(jnp.float32), value_h.astype(jnp.float32)).astype(jnp.bfloat16)
    return (attention_result, logged_total)

def attend_backward(query_h, key_h, value_h, attention_result, d_att, logged_total):
    scale_value = HD ** (-0.5)
    scores = jnp.einsum('qhd,khd->hqk', query_h.astype(jnp.float32), key_h.astype(jnp.float32)) * scale_value
    probs = jnp.exp(scores - logged_total)
    probs_low = probs.astype(jnp.bfloat16)
    d_value = jnp.einsum('hqk,qhd->khd', probs_low.astype(jnp.float32), d_att.astype(jnp.float32))
    d_probs = jnp.einsum('qhd,khd->hqk', d_att.astype(jnp.float32), value_h.astype(jnp.float32))
    delta = lax.optimization_barrier(jnp.sum(d_att.astype(jnp.float32) * attention_result.astype(jnp.float32), -1))
    d_scores = (probs * (d_probs - jnp.transpose(delta)[:, :, None]) * scale_value).astype(jnp.bfloat16)
    d_query = jnp.einsum('hqk,khd->qhd', d_scores.astype(jnp.float32), key_h.astype(jnp.float32))
    d_key = jnp.einsum('hqk,qhd->khd', d_scores.astype(jnp.float32), query_h.astype(jnp.float32))
    return (d_query, d_key, d_value)

def adam_update(param, running_gradient, moments, decay):
    first = BETA_ONE * moments[0] + (1.0 - BETA_ONE) * running_gradient
    second = BETA_TWO * moments[1] + (1.0 - BETA_TWO) * running_gradient * running_gradient
    fix_one = 1.0 - BETA_ONE ** STEP
    fix_two = 1.0 - BETA_TWO ** STEP
    update = first / fix_one / (jnp.sqrt(second / fix_two) + ADAM_EPS) + decay * param
    return (param - LEARN_RATE * update, jnp.stack([first, second]))

def reference(tokens, cotangent, image_counts, w_qkv, w_out, w_fc1, w_fc2, vec_small, fc1_bias, mom_qkv, mom_out, mom_fc1, mom_fc2, mom_vec, mom_bias):
    live_all = jnp.stack([jnp.ones_like(image_counts), (image_counts == 2).astype(jnp.int32)], 1).reshape(-1).astype(jnp.float32)

    def run_slot(totals, inputs):
        slot_tokens, slot_cot, slot_live = inputs
        hidden_state = slot_tokens.astype(jnp.float32)
        saved_tensors = []
        for layer_number in range(LAYERS):
            vector_rows = vec_small[layer_number]
            projection_weight = w_qkv[layer_number].astype(jnp.bfloat16).reshape(D, 3 * D)
            backward_weight = w_out[layer_number].astype(jnp.bfloat16)
            first_weight = w_fc1[layer_number].astype(jnp.bfloat16)
            second_weight = w_fc2[layer_number].astype(jnp.bfloat16)
            first_centered_scaled, first_inverse_deviation = layernorm_forward(hidden_state)
            first_normalized = (first_centered_scaled * vector_rows[0] + vector_rows[1]).astype(jnp.bfloat16)
            proj_out = jnp.dot(first_normalized, projection_weight, preferred_element_type=jnp.float32).reshape(SEQ, 3, D)
            query_matrix_rows = (proj_out[:, 0] + vector_rows[2]).astype(jnp.bfloat16)
            key_matrix_rows = proj_out[:, 1].astype(jnp.bfloat16)
            value_matrix_rows = (proj_out[:, 2] + vector_rows[3]).astype(jnp.bfloat16)
            attention_result, logged_total = attend_forward(split_heads(query_matrix_rows), split_heads(key_matrix_rows), split_heads(value_matrix_rows))
            attention_result = attention_result.reshape(SEQ, D)
            middle_state = hidden_state + jnp.dot(attention_result, backward_weight.T, preferred_element_type=jnp.float32) + vector_rows[4]
            second_centered_scaled, second_inverse_deviation = layernorm_forward(middle_state)
            second_normalized = (second_centered_scaled * vector_rows[5] + vector_rows[6]).astype(jnp.bfloat16)
            preactivation = jnp.dot(second_normalized, first_weight, preferred_element_type=jnp.float32) + fc1_bias[layer_number]
            activation_narrow = gelu_value(preactivation).astype(jnp.bfloat16)
            new_hidden = middle_state + jnp.dot(activation_narrow, second_weight.T, preferred_element_type=jnp.float32) + vector_rows[7]
            saved_tensors.append((projection_weight, backward_weight, first_weight, second_weight, first_centered_scaled, first_inverse_deviation, first_normalized, query_matrix_rows, key_matrix_rows, value_matrix_rows, attention_result, logged_total, second_centered_scaled, second_inverse_deviation, second_normalized, preactivation, activation_narrow))
            hidden_state = new_hidden
        running_gradient = slot_cot * slot_live
        layer_grads = [None] * LAYERS
        for layer_number in reversed(range(LAYERS)):
            vector_rows = vec_small[layer_number]
            projection_weight, backward_weight, first_weight, second_weight, first_centered_scaled, first_inverse_deviation, first_normalized, query_matrix_rows, key_matrix_rows, value_matrix_rows, attention_result, logged_total, second_centered_scaled, second_inverse_deviation, second_normalized, preactivation, activation_narrow = saved_tensors[layer_number]
            grad_low = running_gradient.astype(jnp.bfloat16)
            g_fc2 = jnp.dot(grad_low.T, activation_narrow, preferred_element_type=jnp.float32)
            g_bias_two = lax.optimization_barrier(jnp.sum(running_gradient, 0))
            d_pre = jnp.dot(grad_low, second_weight, preferred_element_type=jnp.float32) * gelu_slope(preactivation)
            d_pre_low = d_pre.astype(jnp.bfloat16)
            g_fc1 = jnp.dot(second_normalized.T, d_pre_low, preferred_element_type=jnp.float32)
            g_fc1_bias = lax.optimization_barrier(jnp.sum(d_pre, 0))
            second_normed_gradient = jnp.dot(d_pre_low, first_weight.T, preferred_element_type=jnp.float32)
            middle_gradient, second_gain_gradient, second_shift_gradient = layernorm_backward(second_normed_gradient, second_centered_scaled, second_inverse_deviation, vector_rows[5], running_gradient)
            mid_low = middle_gradient.astype(jnp.bfloat16)
            g_out = jnp.dot(mid_low.T, attention_result, preferred_element_type=jnp.float32)
            g_bias_out = lax.optimization_barrier(jnp.sum(middle_gradient, 0))
            d_att = jnp.dot(mid_low, backward_weight, preferred_element_type=jnp.float32).astype(jnp.bfloat16)
            d_query, d_key, d_value = attend_backward(split_heads(query_matrix_rows), split_heads(key_matrix_rows), split_heads(value_matrix_rows), split_heads(attention_result), split_heads(d_att), logged_total)
            d_query = d_query.reshape(SEQ, D)
            d_key = d_key.reshape(SEQ, D)
            d_value = d_value.reshape(SEQ, D)
            d_proj = jnp.stack([d_query, d_key, d_value], axis=1).astype(jnp.bfloat16).reshape(SEQ, 3 * D)
            g_qkv = jnp.dot(first_normalized.T, d_proj, preferred_element_type=jnp.float32).reshape(D, 3, D)
            first_normed_gradient = jnp.dot(d_proj, projection_weight.T, preferred_element_type=jnp.float32)
            running_gradient, first_gain_gradient, first_shift_gradient = layernorm_backward(first_normed_gradient, first_centered_scaled, first_inverse_deviation, vector_rows[0], middle_gradient)
            g_vec = jnp.stack([first_gain_gradient, first_shift_gradient, lax.optimization_barrier(jnp.sum(d_query, 0)), lax.optimization_barrier(jnp.sum(d_value, 0)), g_bias_out, second_gain_gradient, second_shift_gradient, g_bias_two])
            layer_grads[layer_number] = (g_qkv, g_out, g_fc1, g_fc2, g_vec, g_fc1_bias)
        stacked = tuple((jnp.stack([entry[which] for entry in layer_grads]) for which in range(6)))
        totals = tuple((total + part for total, part in zip(totals, stacked)))
        return (totals, (hidden_state * slot_live, running_gradient * slot_live))
    zero_totals = (jnp.zeros((LAYERS, D, 3, D), jnp.float32), jnp.zeros((LAYERS, D, D), jnp.float32), jnp.zeros((LAYERS, D, FF), jnp.float32), jnp.zeros((LAYERS, D, FF), jnp.float32), jnp.zeros((LAYERS, 8, D), jnp.float32), jnp.zeros((LAYERS, FF), jnp.float32))
    totals, (output, input_grad) = lax.scan(run_slot, zero_totals, (tokens, cotangent, live_all))
    params = (w_qkv, w_out, w_fc1, w_fc2, vec_small, fc1_bias)
    moments = (mom_qkv, mom_out, mom_fc1, mom_fc2, mom_vec, mom_bias)
    decays = (WEIGHT_DECAY, WEIGHT_DECAY, WEIGHT_DECAY, WEIGHT_DECAY, 0.0, 0.0)
    results = [adam_update(param, grad_total, moment, decay) for param, grad_total, moment, decay in zip(params, totals, moments, decays)]
    return (output, input_grad, totals[0], totals[1], totals[2], totals[3], totals[4], totals[5], results[0][0], results[1][0], results[2][0], results[3][0], results[4][0], results[5][0], results[0][1], results[1][1], results[2][1], results[3][1], results[4][1], results[5][1])
```

```python
import jax
import jax.numpy as jnp
from jax import lax
from jax.sharding import PartitionSpec as P

D = 1024
HEADS = 16
LAYERS = 2
STEP = 10


NORM_EPS = 1e-06
ROOT_HALF = 0.7071067811865476
INV_ROOT_TWO_PI = 0.3989422804014327
LEARN_RATE = 0.01
BETA_ONE = 0.9
BETA_TWO = 0.999
ADAM_EPS = 1e-08
WEIGHT_DECAY = 0.05
CONTRACT_LAST = (((1,), (1,)), ((), ()))
CONTRACT_FIRST = (((0,), (0,)), ((), ()))


def gelu_value(preactivation):
    return 0.5 * preactivation * (1.0 + jax.scipy.special.erf(preactivation * ROOT_HALF))


def gelu_slope(preactivation):
    return (
        0.5 * (1.0 + jax.scipy.special.erf(preactivation * ROOT_HALF))
        + preactivation * jnp.exp(-0.5 * preactivation * preactivation) * INV_ROOT_TWO_PI
    )


def norm_full(hidden_low, gain_full, shift_full):
    wide = hidden_low.astype(jnp.float32)
    mean_row = jnp.mean(wide, -1, keepdims=True)
    spread = jnp.mean(wide * wide, -1, keepdims=True) - mean_row * mean_row
    inv_std = lax.rsqrt(spread + NORM_EPS)
    normalized = ((wide - mean_row) * inv_std * gain_full + shift_full).astype(jnp.bfloat16)
    return normalized, mean_row, inv_std


def share_features(local_rows):
    return lax.all_gather(local_rows, "tensor", axis=1, tiled=True)


def sum_branch(partial_rows):
    return lax.psum_scatter(
        partial_rows.astype(jnp.bfloat16), "tensor", scatter_dimension=1, tiled=True
    ).astype(jnp.float32)


def sum_with_totals(partial_rows, hidden_low, mean_row, inv_std, gain_full):
    rows, width = partial_rows.shape
    parts = lax.axis_size("tensor")
    chunk = width // parts
    d_hat = partial_rows * gain_full
    normed = (hidden_low.astype(jnp.float32) - mean_row) * inv_std
    sums = jnp.concatenate([jnp.sum(d_hat, -1), jnp.sum(d_hat * normed, -1)])
    extra = -(-2 * rows // (16 * chunk)) * 16
    sums = jnp.pad(sums, (0, extra * chunk - 2 * rows)).reshape(extra, chunk)
    operand = jnp.concatenate(
        [
            partial_rows.astype(jnp.bfloat16),
            jnp.tile(sums.astype(jnp.bfloat16), (1, parts)),
        ]
    )
    summed = lax.psum_scatter(operand, "tensor", scatter_dimension=1, tiled=True).astype(
        jnp.float32
    )
    flat = summed[rows:].reshape(-1)
    return summed[:rows], flat[:rows, None], flat[rows : 2 * rows, None]


def norm_back(d_normed, total_plain, total_normed, normed, inv_std, gain, carried):
    d_hat = d_normed * gain
    grad_in = carried + inv_std * (d_hat - total_plain / D - normed * total_normed / D)
    return (grad_in, jnp.sum(d_normed * normed, 0), jnp.sum(d_normed, 0))


def swap_dp(value, bit):
    count = lax.axis_size("dp")
    return lax.ppermute(value, "dp", [(i, i ^ bit) for i in range(count)])


def dp_bits():
    count = lax.axis_size("dp")
    return [1 << i for i in range(count.bit_length() - 1)]


def gather_rows(shard):
    count = lax.axis_size("dp")
    me = lax.axis_index("dp")
    pieces = {0: shard}
    for bit in reversed(dp_bits()):
        for offset in sorted(pieces):
            pieces[offset | bit] = swap_dp(pieces[offset], bit)
    whole = jnp.zeros((count,) + shard.shape, shard.dtype)
    for offset in range(count):
        whole = lax.dynamic_update_index_in_dim(whole, pieces[offset], me ^ offset, 0)
    return whole.reshape((count * shard.shape[0],) + shard.shape[1:])


def scatter_rows(parts):
    count = lax.axis_size("dp")
    me = lax.axis_index("dp")
    share = parts[0].shape[0] // count
    pieces = {}
    for offset in range(count):
        start = (me ^ offset) * share
        pieces[offset] = jnp.concatenate(
            [lax.dynamic_slice_in_dim(part, start, share, 0) for part in parts], axis=1
        )
    for bit in dp_bits():
        kept = {}
        for offset in sorted(pieces):
            if not offset & bit:
                arrived = swap_dp(pieces[offset | bit], bit)
                kept[offset] = (
                    pieces[offset].astype(jnp.float32) + arrived.astype(jnp.float32)
                )
        if len(kept) > 1:
            kept = {k: v.astype(jnp.bfloat16) for k, v in kept.items()}
        pieces = kept
    return pieces[0]


def sum_dp(value):
    for bit in dp_bits():
        value = value + swap_dp(value, bit)
    return value


def fetch_weights(w_qkv, w_out, w_fc1, w_fc2, layer_number):
    rows = w_qkv.shape[1]
    chunk = w_out.shape[2]
    attn = jnp.concatenate(
        [w_qkv[layer_number].reshape(rows, 3 * chunk), w_out[layer_number]], axis=1
    ).astype(jnp.bfloat16)
    return (
        gather_rows(attn),
        gather_rows(w_fc1[layer_number].astype(jnp.bfloat16)),
        gather_rows(w_fc2[layer_number].astype(jnp.bfloat16)),
    )


def attend_forward(query_h, key_h, value_h, attn_scale):
    scores = (
        jnp.einsum("bqhd,bkhd->bhqk", query_h, key_h, preferred_element_type=jnp.float32)
        * attn_scale
    )
    top_score = jnp.max(scores, -1, keepdims=True)
    logged_total = top_score + jnp.log(jnp.sum(jnp.exp(scores - top_score), -1, keepdims=True))
    probs = jnp.exp(scores - logged_total).astype(jnp.bfloat16)
    attention_result = jnp.einsum(
        "bhqk,bkhd->bqhd", probs, value_h, preferred_element_type=jnp.float32
    ).astype(jnp.bfloat16)
    return (attention_result, logged_total)


def attend_backward(query_h, key_h, value_h, attention_result, d_att, logged_total, attn_scale):
    scores = (
        jnp.einsum("bqhd,bkhd->bhqk", query_h, key_h, preferred_element_type=jnp.float32)
        * attn_scale
    )
    probs = jnp.exp(scores - logged_total)
    probs_low = probs.astype(jnp.bfloat16)
    d_value = jnp.einsum("bhqk,bqhd->bkhd", probs_low, d_att, preferred_element_type=jnp.float32)
    d_probs = jnp.einsum("bqhd,bkhd->bhqk", d_att, value_h, preferred_element_type=jnp.float32)
    delta = jnp.sum(d_att.astype(jnp.float32) * attention_result.astype(jnp.float32), -1)
    d_scores = (probs * (d_probs - jnp.swapaxes(delta, 1, 2)[..., None]) * attn_scale).astype(
        jnp.bfloat16
    )
    d_query = jnp.einsum("bhqk,bkhd->bqhd", d_scores, key_h, preferred_element_type=jnp.float32)
    d_key = jnp.einsum("bhqk,bqhd->bkhd", d_scores, query_h, preferred_element_type=jnp.float32)
    return (d_query, d_key, d_value)


def adam_update(param, running_gradient, moments, decay):
    first = BETA_ONE * moments[0] + (1.0 - BETA_ONE) * running_gradient
    second = BETA_TWO * moments[1] + (1.0 - BETA_TWO) * running_gradient * running_gradient
    fix_one = 1.0 - BETA_ONE**STEP
    fix_two = 1.0 - BETA_TWO**STEP
    update = first / fix_one / (jnp.sqrt(second / fix_two) + ADAM_EPS) + decay * param
    return (param - LEARN_RATE * update, jnp.stack([first, second]))


def on_device(
    tokens,
    cotangent,
    image_counts,
    w_qkv,
    w_out,
    w_fc1,
    w_fc2,
    vec_small,
    fc1_bias,
    mom_qkv,
    mom_out,
    mom_fc1,
    mom_fc2,
    mom_vec,
    mom_bias,
):
    slot_count, seq_len, feat_width = tokens.shape
    tok_rows = slot_count * seq_len
    heads_here = HEADS // lax.axis_size("tensor")
    head_dim = feat_width // heads_here
    attn_scale = head_dim ** (-0.5)
    row_number = lax.broadcasted_iota(jnp.int32, (tok_rows, 1), 0)
    row_live = jnp.where((row_number < seq_len) | (image_counts[0] == 2), 1.0, 0.0)
    vec_full = lax.all_gather(vec_small, "tensor", axis=2, tiled=True)

    def to_heads(matrix):
        return matrix.reshape(slot_count, seq_len, heads_here, head_dim)

    hidden_low = tokens.reshape(tok_rows, feat_width)
    hidden_state = hidden_low.astype(jnp.float32)
    fetched = [fetch_weights(w_qkv, w_out, w_fc1, w_fc2, n) for n in range(LAYERS)]
    qkv_width = 3 * feat_width
    saved_tensors = []
    for layer_number in range(LAYERS):
        attn_weight, first_weight, second_weight = fetched[layer_number]
        qkv_weight = attn_weight[:, :qkv_width]
        out_weight = attn_weight[:, qkv_width:]
        vector_rows = vec_small[layer_number]
        full_rows = vec_full[layer_number]
        first_low = share_features(hidden_state.astype(jnp.bfloat16))
        first_normalized, first_mean, first_inv = norm_full(first_low, full_rows[0], full_rows[1])
        first_hat = (hidden_state - first_mean) * first_inv
        proj_out = jnp.dot(first_normalized, qkv_weight, preferred_element_type=jnp.float32)
        query_rows = (proj_out[:, :feat_width] + vector_rows[2]).astype(jnp.bfloat16)
        key_rows = proj_out[:, feat_width : 2 * feat_width].astype(jnp.bfloat16)
        value_rows = (proj_out[:, 2 * feat_width :] + vector_rows[3]).astype(jnp.bfloat16)
        attention_result, logged_total = attend_forward(
            to_heads(query_rows), to_heads(key_rows), to_heads(value_rows), attn_scale
        )
        attention_result = attention_result.reshape(tok_rows, feat_width)
        if layer_number == LAYERS - 1:
            last_gradient = cotangent.reshape(tok_rows, feat_width) * row_live
            last_low, first_normalized = lax.optimization_barrier(
                (last_gradient.astype(jnp.bfloat16), first_normalized)
            )
            last_full, attention_result = lax.optimization_barrier(
                (share_features(last_low), attention_result)
            )
        attn_branch = sum_branch(
            lax.dot_general(
                attention_result, out_weight, CONTRACT_LAST, preferred_element_type=jnp.float32
            )
        )
        middle_state = hidden_state + attn_branch + vector_rows[4]
        second_low = share_features(middle_state.astype(jnp.bfloat16))
        second_normalized, second_mean, second_inv = norm_full(
            second_low, full_rows[5], full_rows[6]
        )
        second_hat = (middle_state - second_mean) * second_inv
        preactivation = (
            jnp.dot(second_normalized, first_weight, preferred_element_type=jnp.float32)
            + fc1_bias[layer_number]
        )
        activation_narrow = gelu_value(preactivation).astype(jnp.bfloat16)
        branch_two = lax.dot_general(
            activation_narrow, second_weight, CONTRACT_LAST, preferred_element_type=jnp.float32
        )
        saved_tensors.append(
            (
                first_low,
                first_mean,
                first_inv,
                first_hat,
                first_normalized,
                query_rows,
                key_rows,
                value_rows,
                attention_result,
                logged_total,
                second_low,
                second_mean,
                second_inv,
                second_hat,
                second_normalized,
                preactivation,
                activation_narrow,
            )
        )
        if layer_number < LAYERS - 1:
            hidden_state = middle_state + sum_branch(branch_two) + vector_rows[7]
    running_gradient = last_gradient
    big_grads = [None] * LAYERS
    vec_grads = [None] * LAYERS
    bias_grads = [None] * LAYERS
    for layer_number in reversed(range(LAYERS)):
        attn_weight, first_weight, second_weight = fetched[layer_number]
        qkv_weight = attn_weight[:, :qkv_width]
        out_weight = attn_weight[:, qkv_width:]
        vector_rows = vec_small[layer_number]
        full_rows = vec_full[layer_number]
        (
            first_low,
            first_mean,
            first_inv,
            first_hat,
            first_normalized,
            query_rows,
            key_rows,
            value_rows,
            attention_result,
            logged_total,
            second_low,
            second_mean,
            second_inv,
            second_hat,
            second_normalized,
            preactivation,
            activation_narrow,
        ) = saved_tensors[layer_number]
        full_grad = last_full
        if layer_number < LAYERS - 1:
            full_grad = share_features(running_gradient.astype(jnp.bfloat16))
        g_bias_two = jnp.sum(running_gradient, 0)
        d_pre = jnp.dot(full_grad, second_weight, preferred_element_type=jnp.float32) * gelu_slope(
            preactivation
        )
        d_pre_low = d_pre.astype(jnp.bfloat16)
        g_fc1_bias = jnp.sum(d_pre, 0)
        second_grad, plain_total, normed_total = sum_with_totals(
            lax.dot_general(
                d_pre_low, first_weight, CONTRACT_LAST, preferred_element_type=jnp.float32
            ),
            second_low,
            second_mean,
            second_inv,
            full_rows[5],
        )
        g_fc2 = lax.dot_general(
            full_grad, activation_narrow, CONTRACT_FIRST, preferred_element_type=jnp.float32
        ).astype(jnp.bfloat16)
        g_fc1 = lax.dot_general(
            second_normalized, d_pre_low, CONTRACT_FIRST, preferred_element_type=jnp.float32
        ).astype(jnp.bfloat16)
        s_fc1 = scatter_rows([g_fc1])
        s_fc2 = scatter_rows([g_fc2])
        middle_gradient, second_gain_gradient, second_shift_gradient = norm_back(
            second_grad,
            plain_total,
            normed_total,
            second_hat,
            second_inv,
            vector_rows[5],
            running_gradient,
        )
        full_mid = share_features(middle_gradient.astype(jnp.bfloat16))
        g_out = lax.dot_general(
            full_mid, attention_result, CONTRACT_FIRST, preferred_element_type=jnp.float32
        ).astype(jnp.bfloat16)
        g_bias_out = jnp.sum(middle_gradient, 0)
        d_att = jnp.dot(full_mid, out_weight, preferred_element_type=jnp.float32).astype(
            jnp.bfloat16
        )
        d_query, d_key, d_value = attend_backward(
            to_heads(query_rows),
            to_heads(key_rows),
            to_heads(value_rows),
            to_heads(attention_result),
            to_heads(d_att),
            logged_total,
            attn_scale,
        )
        if layer_number == LAYERS - 1:
            branch_low, full_mid = lax.optimization_barrier(
                (branch_two.astype(jnp.bfloat16), full_mid)
            )
            last_branch, d_query, d_key, d_value = lax.optimization_barrier(
                (sum_branch(branch_low), d_query, d_key, d_value)
            )
            output = ((middle_state + last_branch + vector_rows[7]) * row_live).reshape(
                tokens.shape
            )
        d_query = d_query.reshape(tok_rows, feat_width)
        d_key = d_key.reshape(tok_rows, feat_width)
        d_value = d_value.reshape(tok_rows, feat_width)
        d_proj = jnp.concatenate(
            [d_query.astype(jnp.bfloat16), d_key.astype(jnp.bfloat16), d_value.astype(jnp.bfloat16)],
            axis=1,
        )
        first_grad, plain_total, normed_total = sum_with_totals(
            lax.dot_general(
                d_proj, qkv_weight, CONTRACT_LAST, preferred_element_type=jnp.float32
            ),
            first_low,
            first_mean,
            first_inv,
            full_rows[0],
        )
        g_qkv = lax.dot_general(
            first_normalized, d_proj, CONTRACT_FIRST, preferred_element_type=jnp.float32
        ).astype(jnp.bfloat16)
        s_attn = scatter_rows([g_qkv, g_out])
        running_gradient, first_gain_gradient, first_shift_gradient = norm_back(
            first_grad,
            plain_total,
            normed_total,
            first_hat,
            first_inv,
            vector_rows[0],
            middle_gradient,
        )
        vec_grads[layer_number] = jnp.stack(
            [
                first_gain_gradient,
                first_shift_gradient,
                jnp.sum(d_query, 0),
                jnp.sum(d_value, 0),
                g_bias_out,
                second_gain_gradient,
                second_shift_gradient,
                g_bias_two,
            ]
        )
        bias_grads[layer_number] = g_fc1_bias
        big_grads[layer_number] = (
            s_attn[:, :qkv_width].reshape(-1, 3, feat_width),
            s_attn[:, qkv_width:],
            s_fc1,
            s_fc2,
        )
    input_grad = (running_gradient * row_live).reshape(tokens.shape)
    stacked = tuple(jnp.stack([entry[which] for entry in big_grads]) for which in range(4))
    vec_rows = vec_small.shape[0] * vec_small.shape[1]
    small = sum_dp(
        jnp.concatenate(
            [
                jnp.stack(vec_grads).reshape(vec_rows, feat_width),
                jnp.stack(bias_grads).reshape(-1, feat_width),
            ]
        )
    )
    small_sums = (small[:vec_rows].reshape(vec_small.shape), small[vec_rows:].reshape(fc1_bias.shape))
    grad_totals = (stacked[0], stacked[1], stacked[2], stacked[3], small_sums[0], small_sums[1])
    params = (w_qkv, w_out, w_fc1, w_fc2, vec_small, fc1_bias)
    moments = (mom_qkv, mom_out, mom_fc1, mom_fc2, mom_vec, mom_bias)
    decays = (WEIGHT_DECAY, WEIGHT_DECAY, WEIGHT_DECAY, WEIGHT_DECAY, 0.0, 0.0)
    results = [
        adam_update(param, grad_total, moment, decay)
        for param, grad_total, moment, decay in zip(params, grad_totals, moments, decays)
    ]
    return (
        output,
        input_grad,
        grad_totals[0],
        grad_totals[1],
        grad_totals[2],
        grad_totals[3],
        grad_totals[4],
        grad_totals[5],
        results[0][0],
        results[1][0],
        results[2][0],
        results[3][0],
        results[4][0],
        results[5][0],
        results[0][1],
        results[1][1],
        results[2][1],
        results[3][1],
        results[4][1],
        results[5][1],
    )


def solution(mesh):
    return jax.shard_map(
        on_device,
        mesh=mesh,
        in_specs=(
            P("dp", None, "tensor"),
            P("dp", None, "tensor"),
            P("dp"),
            P(None, "dp", None, "tensor"),
            P(None, "dp", "tensor"),
            P(None, "dp", "tensor"),
            P(None, "dp", "tensor"),
            P(None, None, "tensor"),
            P(None, "tensor"),
            P(None, None, "dp", None, "tensor"),
            P(None, None, "dp", "tensor"),
            P(None, None, "dp", "tensor"),
            P(None, None, "dp", "tensor"),
            P(None, None, None, "tensor"),
            P(None, None, "tensor"),
        ),
        out_specs=(
            P("dp", None, "tensor"),
            P("dp", None, "tensor"),
            P(None, "dp", None, "tensor"),
            P(None, "dp", "tensor"),
            P(None, "dp", "tensor"),
            P(None, "dp", "tensor"),
            P(None, None, "tensor"),
            P(None, "tensor"),
            P(None, "dp", None, "tensor"),
            P(None, "dp", "tensor"),
            P(None, "dp", "tensor"),
            P(None, "dp", "tensor"),
            P(None, None, "tensor"),
            P(None, "tensor"),
            P(None, None, "dp", None, "tensor"),
            P(None, None, "dp", "tensor"),
            P(None, None, "dp", "tensor"),
            P(None, None, "dp", "tensor"),
            P(None, None, None, "tensor"),
            P(None, None, "tensor"),
        ),
        check_vma=False,
    )
```
